32 devices in a mesh: groups: 2 (over x), ctx: 16 (over z, y, core).
Axes of the slice: x: 2, y: 2, z: 4, core: 2. Of those that a mesh axis runs over, the one named last changes fastest.
Arguments:
- q_latent: bfloat16 [128, 1536], P(('groups', 'ctx')), parts along dimension 0, may hold values from -64 to 64
- q_gain: float32 [1536], replicated, may hold values from 0.1 to 1.9
- w_uq: bfloat16 [1536, 24576], P(None, 'ctx'), may hold values from -0.15625 to 0.15625
- w_uk: bfloat16 [128, 128, 512], P('ctx'), may hold values from -0.5 to 0.5
- w_uv: bfloat16 [128, 512, 128], P('ctx'), may hold values from -0.25 to 0.25
- w_o: bfloat16 [16384, 7168], P('ctx'), may hold values from -0.046875 to 0.046875
- latent_cache: bfloat16 [65536, 576], P(('groups', 'ctx')), parts along dimension 0, may hold values from -1024 to 1024
- kv_scales: float32 [65536, 4], P(('groups', 'ctx')), parts along dimension 0, may hold values from 0.5 to 2
- selected: int32 [128, 32], P(('groups', 'ctx')), parts along dimension 0, may hold values from 0 to 511, as said below
- counts: int32 [128], P(('groups', 'ctx')), parts along dimension 0, may hold values from 8 to 32
Outputs:
- attn_out: bfloat16 [128, 7168], P(('groups', 'ctx')), parts along dimension 0
The draws below stay inside these ranges and needn't reach their ends.
There are 2 independent parts, one for each index of `groups`. The reference program is written for one: setup_inputs(seed, part) draws one part's arguments, and reference() takes and returns one part's arrays. A program takes and returns all parts, laid end to end along the dimension named above; an argument that names none is the same for every part. Nothing has to cross between parts.
Inputs may be any that keep to these rules, and one draw needn't show every extreme that they name: `selected`: each row lists 32 different block numbers. Over the rows 4 i to 4 i + 4 - 1 (the query tokens of one device) and their first counts entries, at most 8 different listed blocks lie in the range 32 j to 32 j + 31 for any j.
All inputs are finite; a program needn't handle non-finite values.
Results may differ from the reference program's by a relative error of at most 0.01.
The reference program's roundings to bfloat16 on the way count: a program that leaves them out, or rounds other values in their place, can miss the bound.
Values may be sent and summed in bfloat16 or wider, within the bound.
A program may use at most 128 MiB of HBM per device.

```python
import math
import jax
import jax.numpy as jnp
from jax import lax

QL = 1536
H = 128
DN = 128
DR = 64
DC = 512
DV = 128
D = 7168
TOPB = 32
BLK = 64
NT = 4
Q_DEV = 4
NB_DEV = 32
QTOK = 64
NBLK = 512
CTX = 32768
UB = 64
CAP = 8


def draw_q_latent(key, part):
    seeds = jax.random.split(jax.random.fold_in(key, 11), 4)
    values_all = jnp.clip(jax.random.normal(seeds[0], (QTOK, QL), jnp.float32), -6.0, 6.0)
    row_scale = jnp.exp(jax.random.uniform(seeds[2], (QTOK, 1), jnp.float32, math.log(0.3), math.log(3.0)))
    col_scale = jnp.exp(jax.random.uniform(seeds[3], (1, QL), jnp.float32, math.log(0.3), math.log(3.0)))
    return (values_all * row_scale * col_scale).astype(jnp.bfloat16)


def draw_latent_cache(key, part):
    seeds = jax.random.split(jax.random.fold_in(key, 23), 1)
    values_all = jnp.clip(jax.random.normal(seeds[0], (CTX, DC + DR), jnp.float32), -4.0, 4.0)
    return values_all.astype(jnp.bfloat16)


def routing_tables(key):
    seeds = jax.random.split(jax.random.fold_in(key, 7717), 8)
    n_dev = QTOK // Q_DEV
    pool_size = n_dev * CAP
    hot_owner = jax.random.permutation(seeds[0], n_dev) < 2
    hot_slot = jnp.repeat(hot_owner, CAP)
    priority = jax.random.randint(seeds[1], (n_dev, pool_size), 0, 2 ** 20) + jnp.where(hot_slot, 0, 2 ** 20)[None, :]
    priority = priority * pool_size + jnp.arange(pool_size, dtype=jnp.int32)[None, :]
    chosen = jnp.argsort(priority, axis=1)[:, :UB].astype(jnp.int32)
    local_score = jax.random.randint(seeds[2], (n_dev, n_dev, NB_DEV), 0, 2 ** 20) * NB_DEV + jnp.arange(NB_DEV, dtype=jnp.int32)
    local_pick = jnp.argsort(local_score, axis=2)[:, :, :CAP].astype(jnp.int32).reshape(n_dev, pool_size)
    union_blocks = chosen // CAP * NB_DEV + jnp.take_along_axis(local_pick, chosen, axis=1)
    query_score = jax.random.randint(seeds[3], (n_dev, Q_DEV, UB), 0, 2 ** 20) * UB + jnp.arange(UB, dtype=jnp.int32)
    query_perm = jnp.argsort(query_score, axis=2)[:, :, :TOPB].astype(jnp.int32)
    first_query = jax.random.randint(seeds[5], (n_dev,), 0, Q_DEV)
    query_ids = jnp.arange(Q_DEV, dtype=jnp.int32)[None, :]
    is_first = query_ids == first_query[:, None]
    head_slots = jnp.broadcast_to(jnp.arange(TOPB, dtype=jnp.int32)[None, None, :], (n_dev, Q_DEV, TOPB))
    slot_pick = jnp.where(is_first[:, :, None], head_slots, query_perm)
    spread_union = jnp.broadcast_to(union_blocks[:, None, :], (n_dev, Q_DEV, UB))
    selected = jnp.take_along_axis(spread_union, slot_pick, axis=2)
    fewest = max(1, TOPB // 4)
    live_counts = jax.random.randint(seeds[7], (n_dev, Q_DEV), fewest, TOPB + 1)
    live_counts = jnp.where(is_first, TOPB, live_counts)
    return (selected.reshape(QTOK, TOPB).astype(jnp.int32), live_counts.reshape(QTOK).astype(jnp.int32))


def draw_selected(key, part):
    return routing_tables(key)[0]


def draw_counts(key, part):
    return routing_tables(key)[1]


def block_scale(own_key, dims, cuts, smallest, high):
    def one(axis_at, shards_of):
        draws = jax.random.uniform(jax.random.fold_in(jax.random.fold_in(own_key, 6), axis_at), (shards_of,), jnp.float32, smallest / len(cuts), high / len(cuts))
        return jnp.repeat(jnp.exp(draws), dims[axis_at] // shards_of).reshape((-1,) + (1,) * (len(dims) - axis_at - 1))

    loudness = one(*cuts[0])
    for cut in cuts[1:]:
        loudness = loudness * one(*cut)
    return loudness


def gaussian(own_key, extent, deviation, reach, cuts=(), held_as=jnp.bfloat16):
    drawn = deviation * jax.random.normal(own_key, extent, jnp.float32)
    if cuts:
        drawn = drawn * block_scale(own_key, extent, cuts, -0.22, 0.18)
    return jnp.clip(drawn, -reach, reach).astype(held_as)


def setup_inputs(seed: int = 0, part: int = 0) -> dict:
    streams_of = jax.random.split(jax.random.key(seed), 11)
    own_keys = jax.random.split(jax.random.fold_in(streams_of[10], part), 11)
    q_latent = draw_q_latent(jax.random.fold_in(jax.random.fold_in(streams_of[10], part), 71), part)
    q_gain = jnp.clip(1.0 + 0.18 * jax.random.normal(streams_of[1], (QL,), jnp.float32), 0.1, 1.9)
    w_uq = gaussian(streams_of[2], (QL, H * (DN + DR)), QL ** -0.5, 0.15625, ((1, 16),))
    w_uk = gaussian(streams_of[3], (H, DN, DC), DN ** -0.5, 0.5, ((0, 16),))
    w_uv = gaussian(streams_of[4], (H, DC, DV), DC ** -0.5, 0.25, ((0, 16),))
    w_o = gaussian(streams_of[5], (H * DV, D), (H * DV) ** -0.5, 0.046875, ((0, 16),))
    latent_cache = draw_latent_cache(jax.random.fold_in(jax.random.fold_in(streams_of[10], part), 71), part)
    kv_scales = jnp.clip(jnp.exp(math.log(2.0) - 1.3862944 * jax.random.uniform(own_keys[7], (CTX, NT), jnp.float32) ** block_scale(own_keys[7], (CTX, NT), ((0, 16),), -0.2, 0.2)), 0.5, 2.0)
    selected = draw_selected(jax.random.fold_in(jax.random.fold_in(streams_of[10], part), 71), part)
    counts = draw_counts(jax.random.fold_in(jax.random.fold_in(streams_of[10], part), 71), part)
    return dict(q_latent=q_latent, q_gain=q_gain, w_uq=w_uq, w_uk=w_uk, w_uv=w_uv, w_o=w_o, latent_cache=latent_cache, kv_scales=kv_scales, selected=selected, counts=counts)


norm_eps = 1e-06
rope_base = 10000.0

def rotate_rotary(rotary, positions):
    half_width = rotary.shape[-1] // 2
    freq_index = jnp.arange(half_width, dtype=jnp.float32)
    inverse_freq = jnp.exp(freq_index * (-2.0 * math.log(rope_base) / rotary.shape[-1]))
    angles = positions[:, None] * inverse_freq[None, :]
    cosine = jnp.cos(angles)[:, None, :]
    sine = jnp.sin(angles)[:, None, :]
    first_half = rotary[:, :, :half_width]
    second_half = rotary[:, :, half_width:]
    return jnp.concatenate([first_half * cosine - second_half * sine, first_half * sine + second_half * cosine], axis=2)

def reference(q_latent, q_gain, w_uq, w_uk, w_uv, w_o, latent_cache, kv_scales, selected, counts):
    latent_f = q_latent.astype(jnp.float32)
    normed = (latent_f * lax.rsqrt(lax.optimization_barrier(jnp.mean(latent_f * latent_f, axis=1, keepdims=True)) + norm_eps) * q_gain).astype(jnp.bfloat16)
    projected = jnp.dot(normed, w_uq, preferred_element_type=jnp.float32).reshape(QTOK, H, DN + DR)
    content = projected[:, :, :DN].astype(jnp.bfloat16)
    positions = jnp.arange(QTOK, dtype=jnp.float32)
    rotated = rotate_rotary(projected[:, :, DN:], positions).astype(jnp.bfloat16)
    absorbed = jnp.einsum('qhn,hnc->qhc', content.astype(jnp.float32), w_uk.astype(jnp.float32)).astype(jnp.bfloat16)
    queries = jnp.concatenate([absorbed, rotated], axis=2)
    scaled = (latent_cache[:, :DC].astype(jnp.float32) * jnp.repeat(kv_scales, DC // NT, axis=1)).astype(jnp.bfloat16)
    cache_rows = jnp.concatenate([scaled, latent_cache[:, DC:]], axis=1).reshape(NBLK, BLK, DC + DR)
    softmax_scale = 1.0 / math.sqrt(DN + DR)

    def attend(inputs):
        query_row, blocks, live_count = inputs
        key_rows = cache_rows[blocks].reshape(TOPB * BLK, DC + DR).astype(jnp.float32)
        live_tokens = jnp.repeat(jnp.arange(TOPB, dtype=jnp.int32) < live_count, BLK)
        scores = jnp.dot(query_row.astype(jnp.float32), key_rows.T, preferred_element_type=jnp.float32) * softmax_scale
        scores = jnp.where(live_tokens[None, :], scores, -jnp.inf)
        row_peak = lax.optimization_barrier(jnp.max(scores, axis=1, keepdims=True))
        exponent = jnp.exp(scores - row_peak)
        weights = (exponent / lax.optimization_barrier(jnp.sum(exponent, axis=1, keepdims=True))).astype(jnp.bfloat16)
        return jnp.dot(weights.astype(jnp.float32), key_rows[:, :DC], preferred_element_type=jnp.float32).astype(jnp.bfloat16)
    latent_out = lax.map(attend, (queries, selected, counts))
    head_values = jnp.einsum('qhc,hcv->qhv', latent_out.astype(jnp.float32), w_uv.astype(jnp.float32)).astype(jnp.bfloat16)
    head_values = head_values.reshape(QTOK, H * DV)
    return jnp.dot(head_values, w_o, preferred_element_type=jnp.float32).astype(jnp.bfloat16)
```

```python
import functools
import math

import jax
import jax.numpy as jnp
from jax import lax
from jax.experimental import pallas as pl
from jax.experimental.pallas import tpu as pltpu
from jax.sharding import PartitionSpec as P

BLK = 64
SIDE = 2
TILES = 7
LAG = 2
KEY_PIECES = 8
QUERY_PIECES = 4

norm_eps = 1e-06
rope_base = 10000.0
EMPTY = -1e30


def exchange_kernel(
    cache_bits, query_bits, q_ref, gain_ref, sel_ref, scales_ref, w_uq_ref, w_uk_ref, cache_ref,
    keys_ref, rots_ref, q_out_ref, q_rot_ref, sel_out_ref, q_in, gain, scales, raw, w_uq, w_uk,
    normed, lat, rows_x, rows_q, rows_r, q_pack, load_sems, gather_send, gather_recv, key_send,
    key_recv, q_send, q_recv,
):
    n_devices = lat.shape[0]
    me = lax.axis_index("ctx")
    near_bit, far_bit = cache_bits
    q_local, width_q = q_ref.shape
    width_row, span = raw.shape
    n_tiles = scales_ref.shape[0]
    heads, width_content, width_latent = w_uk.shape
    width_rotary = width_row - width_latent
    width_head = width_content + width_rotary
    _, blocks, blk, _ = keys_ref.shape
    n_chunks, groups, rows, _ = q_out_ref.shape
    key_step = blocks // KEY_PIECES
    q_step = groups // QUERY_PIECES
    key_span = span // KEY_PIECES
    tokens = n_devices * q_local
    half = width_rotary // 2

    def peer(bit):
        return me + bit * (1 - 2 * ((me // bit) % 2))

    def key_load(i):
        part = pl.ds(i * key_span, key_span)
        return pltpu.make_async_copy(
            cache_ref.at[:width_latent, part], raw.at[:width_latent, part], load_sems.at[i]
        )

    others = [
        pltpu.make_async_copy(source, target, load_sems.at[KEY_PIECES + k])
        for k, (source, target) in enumerate(
            (
                (q_ref, q_in),
                (gain_ref, gain),
                (scales_ref, scales),
                (cache_ref.at[width_latent:], raw.at[width_latent:]),
                (w_uq_ref, w_uq),
                (w_uk_ref, w_uk),
            )
        )
    ]
    q_load, gain_load, scales_load, rot_load, w_uq_load, w_uk_load = others
    q_load.start()
    gain_load.start()
    scales_load.start()
    rot_load.start()
    for i in range(KEY_PIECES):
        key_load(i).start()
    w_uq_load.start()
    w_uk_load.start()
    barrier = pltpu.get_barrier_semaphore()
    for d in range(1, n_devices):
        pl.semaphore_signal(barrier, inc=1, device_id={"ctx": (me + d) % n_devices})

    q_load.wait()
    gain_load.wait()
    latent = q_in[...].astype(jnp.float32)
    mean = jnp.mean(latent * latent, axis=1, keepdims=True)
    normed[...] = (latent * lax.rsqrt(mean + norm_eps) * gain[...]).astype(jnp.bfloat16)
    rot_load.wait()
    halfway = span // 2
    stacked = jnp.concatenate(
        [raw[width_latent:, :halfway], raw[width_latent:, halfway:]], axis=0
    ).astype(jnp.float32)
    rots_ref[0, : blocks // 2] = stacked.T.astype(jnp.bfloat16).reshape(blocks // 2, blk, -1)

    def key_copy(kind, i):
        source, target, bit = ((0, 1, near_bit), (0, 2, far_bit), (2, 3, near_bit))[kind]
        if i == KEY_PIECES:
            ref, piece = rots_ref, pl.ds(0, blocks // 2)
        else:
            ref, piece = keys_ref, pl.ds(i * key_step, key_step)
        return pltpu.make_async_remote_copy(
            src_ref=ref.at[source, piece],
            dst_ref=ref.at[target, piece],
            send_sem=key_send.at[kind, i],
            recv_sem=key_recv.at[kind, i],
            device_id={"ctx": peer(bit)},
        )

    def scale_piece(i):
        key_load(i).wait()
        part = slice(i * key_span, (i + 1) * key_span)
        deep = width_latent // n_tiles
        for c in range(n_tiles):
            strip = (
                raw[c * deep : (c + 1) * deep, part].astype(jnp.float32) * scales[c : c + 1, part]
            )
            keys_ref[0, i * key_step : (i + 1) * key_step, :, c * deep : (c + 1) * deep] = (
                strip.T.astype(jnp.bfloat16).reshape(key_step, blk, deep)
            )

    pl.semaphore_wait(barrier, n_devices - 1)
    gathers = []
    for d in range(1, n_devices):
        for k, (source, target) in enumerate(((normed, lat), (sel_ref, sel_out_ref))):
            gathers.append(
                pltpu.make_async_remote_copy(
                    src_ref=source,
                    dst_ref=target.at[me],
                    send_sem=gather_send.at[k, d],
                    recv_sem=gather_recv.at[k, d],
                    device_id={"ctx": (me + d) % n_devices},
                )
            )
    for copy in gathers:
        copy.start()
    key_copy(1, KEY_PIECES).start()
    key_copy(0, KEY_PIECES).start()
    lat[me] = normed[...]
    sel_out_ref[me] = sel_ref[...]
    scales_load.wait()
    for i in range(KEY_PIECES):
        scale_piece(i)
        key_copy(1, i).start()
        key_copy(0, i).start()
    lane = lax.broadcasted_iota(jnp.int32, (tokens, width_rotary), 1)
    position = lax.broadcasted_iota(jnp.int32, (tokens, width_rotary), 0).astype(jnp.float32)
    frequency = jnp.exp((lane % half).astype(jnp.float32) * (-2.0 * math.log(rope_base) / width_rotary))
    cosine = jnp.cos(position * frequency)
    sine = jnp.sin(position * frequency) * jnp.where(lane < half, -1.0, 1.0)
    w_uq_load.wait()
    w_uk_load.wait()
    for copy in gathers:
        copy.wait()
    for d in range(n_devices):
        rows_x[d * q_local : (d + 1) * q_local] = lat[d].astype(jnp.float32)
    projected = jnp.dot(
        rows_x[...].astype(jnp.bfloat16), w_uq[...], preferred_element_type=jnp.float32
    )
    for h in range(heads):
        head = projected[:, h * width_head : (h + 1) * width_head]
        rotary = head[:, width_content:]
        swapped = jnp.concatenate([rotary[:, half:], rotary[:, :half]], axis=1)
        rows_r[:, h, :] = rotary * cosine + swapped * sine
    pairs = jnp.concatenate([rows_r[: tokens // 2], rows_r[tokens // 2 :]], axis=2)
    q_pack[0] = pairs.reshape(groups // 2, rows, 2 * width_rotary).astype(jnp.bfloat16)

    stages = [(i, bit) for i, bit in enumerate(reversed(query_bits))]

    def q_copy(stage, source, j):
        target = 2**stage + source
        if j == QUERY_PIECES:
            ref, piece = q_pack, pl.ds(0, groups // 2)
        else:
            ref, piece = q_out_ref, pl.ds(j * q_step, q_step)
        return pltpu.make_async_remote_copy(
            src_ref=ref.at[source, piece],
            dst_ref=ref.at[target, piece],
            send_sem=q_send.at[target, j],
            recv_sem=q_recv.at[target, j],
            device_id={"ctx": peer(stages[stage][1])},
        )

    for h in range(heads):
        rows_q[:, h, :] = jnp.dot(
            projected[:, h * width_head : h * width_head + width_content].astype(jnp.bfloat16),
            w_uk[h],
            preferred_element_type=jnp.float32,
        )
    for j in range(QUERY_PIECES):
        first = j * q_step
        q_out_ref[0, first : first + q_step] = (
            rows_q[first * q_local : (first + q_step) * q_local]
            .reshape(q_step, rows, width_latent)
            .astype(jnp.bfloat16)
        )
        for stage, _ in stages:
            q_copy(stage, 0, j).start()
    for stage, _ in stages:
        q_copy(stage, 0, QUERY_PIECES).start()

    low_lane = lax.broadcasted_iota(jnp.int32, (groups // 2, rows, 2 * width_rotary), 2) < width_rotary

    def unpack_query(slot):
        pair = q_pack[slot].astype(jnp.float32)
        rolled = jnp.concatenate([pair[:, :, width_rotary:], pair[:, :, :width_rotary]], axis=2)
        q_rot_ref[slot, : groups // 2] = jnp.where(low_lane, pair, 0.0).astype(jnp.bfloat16)
        q_rot_ref[slot, groups // 2 :] = jnp.where(low_lane, rolled, 0.0).astype(jnp.bfloat16)

    def unpack_rots(slot):
        pair = rots_ref[slot, : blocks // 2].astype(jnp.float32)
        rolled = jnp.concatenate([pair[:, :, width_rotary:], pair[:, :, :width_rotary]], axis=2)
        rots_ref[slot, blocks // 2 :] = rolled.astype(jnp.bfloat16)

    unpack_query(0)
    unpack_rots(0)
    key_copy(0, KEY_PIECES).wait_recv()
    unpack_rots(1)
    arrivals = [(0.0, "key", KEY_PIECES, 0)]
    for i in range(KEY_PIECES):
        arrivals.append(((i + 1.0) / KEY_PIECES, "key", i, 0))
    for j in range(QUERY_PIECES + 1):
        for slot in range(1, n_chunks):
            at = 0.15 + 0.85 * (slot * QUERY_PIECES + j + 1.0) / (n_chunks * QUERY_PIECES)
            arrivals.append((at, "query", slot, j))
    for _, what, a, b in sorted(arrivals):
        if what == "key":
            key_copy(1, a).wait_recv()
            key_copy(2, a).start()
            if a == KEY_PIECES:
                unpack_rots(2)
        else:
            stage = a.bit_length() - 1
            q_copy(stage, a - 2**stage, b).wait_recv()
            for later in range(stage + 1, len(stages)):
                q_copy(later, a, b).start()
            if b == QUERY_PIECES:
                unpack_query(a)
    key_copy(2, KEY_PIECES).wait_recv()
    unpack_rots(3)
    for i in range(KEY_PIECES + 1):
        if i < KEY_PIECES:
            key_copy(0, i).wait_recv()
            key_copy(2, i).wait_recv()
        for kind in range(3):
            key_copy(kind, i).wait_send()
    for j in range(QUERY_PIECES + 1):
        for slot in range(1, n_chunks):
            stage = slot.bit_length() - 1
            q_copy(stage, slot - 2**stage, j).wait_send()


def exchange(
    cache_bits, query_bits, n_devices, q_latent, q_gain, listed, w_uq, w_uk, latent_cache, kv_scales
):
    q_local, width_q = q_latent.shape
    heads, _, width_latent = w_uk.shape
    span, width_row = latent_cache.shape
    blocks = span // BLK
    tokens = n_devices * q_local
    groups = n_devices
    n_chunks = 2 ** len(query_bits)
    rows = q_local * heads
    width_rotary = width_row - width_latent
    vmem = pl.BlockSpec(memory_space=pltpu.VMEM)
    any_space = pl.BlockSpec(memory_space=pl.ANY)
    return pl.pallas_call(
        functools.partial(exchange_kernel, cache_bits, query_bits),
        out_shape=[
            jax.ShapeDtypeStruct((4, blocks, BLK, width_latent), jnp.bfloat16),
            jax.ShapeDtypeStruct((4, blocks, BLK, 2 * width_rotary), jnp.bfloat16),
            jax.ShapeDtypeStruct((n_chunks, groups, rows, width_latent), jnp.bfloat16),
            jax.ShapeDtypeStruct((n_chunks, groups, rows, 2 * width_rotary), jnp.bfloat16),
            jax.ShapeDtypeStruct((n_devices,) + listed.shape, jnp.int32),
        ],
        in_specs=[any_space] * 2 + [vmem] + [any_space] * 4,
        out_specs=[vmem] * 5,
        scratch_shapes=[
            pltpu.VMEM(q_latent.shape, jnp.bfloat16),
            pltpu.VMEM((1, width_q), jnp.float32),
            pltpu.VMEM(kv_scales.shape[::-1], jnp.float32),
            pltpu.VMEM((width_row, span), jnp.bfloat16),
            pltpu.VMEM(w_uq.shape, jnp.bfloat16),
            pltpu.VMEM(w_uk.shape, jnp.bfloat16),
            pltpu.VMEM(q_latent.shape, jnp.bfloat16),
            pltpu.VMEM((n_devices,) + q_latent.shape, jnp.bfloat16),
            pltpu.VMEM((tokens, width_q), jnp.float32),
            pltpu.VMEM((tokens, heads, width_latent), jnp.float32),
            pltpu.VMEM((tokens, heads, width_rotary), jnp.float32),
            pltpu.VMEM((n_chunks, groups // 2, rows, 2 * width_rotary), jnp.bfloat16),
            pltpu.SemaphoreType.DMA((KEY_PIECES + 6,)),
            pltpu.SemaphoreType.DMA((2, n_devices)),
            pltpu.SemaphoreType.DMA((2, n_devices)),
            pltpu.SemaphoreType.DMA((3, KEY_PIECES + 1)),
            pltpu.SemaphoreType.DMA((3, KEY_PIECES + 1)),
            pltpu.SemaphoreType.DMA((n_chunks, QUERY_PIECES + 1)),
            pltpu.SemaphoreType.DMA((n_chunks, QUERY_PIECES + 1)),
        ],
        compiler_params=pltpu.CompilerParams(
            collective_id=0, has_side_effects=True, vmem_limit_bytes=48 * 2**20
        ),
        name="exchange",
    )(q_latent, q_gain[None, :], listed, kv_scales.T, w_uq, w_uk, latent_cache.T)


def reduce_kernel(
    query_bits, heads, cap, scale, list_ref, keys_ref, rots_ref, q_ref, q_rot_ref, out_ref, mine,
    logs, *bufs
):
    n_stages = len(query_bits)
    recvs, log_recvs = bufs[:n_stages], bufs[n_stages : 2 * n_stages]
    send_sems, recv_sems = bufs[2 * n_stages :]
    me = lax.axis_index("ctx")
    n_chunks, groups, rows, width = q_ref.shape
    n_parts = keys_ref.shape[0]
    n_batches = groups // SIDE
    total_rows = n_chunks * rows
    tokens = rows // heads
    base = 2**tokens
    span = cap * BLK
    peers = [me + bit * (1 - 2 * ((me // bit) % 2)) for bit in query_bits]
    barrier = pltpu.get_barrier_semaphore()
    for other in peers:
        pl.semaphore_signal(barrier, inc=1, device_id={"ctx": other})
    pl.semaphore_wait(barrier, n_stages)

    token_of_row = (lax.broadcasted_iota(jnp.int32, (total_rows, 1), 0) // heads) % tokens
    row_bit = lax.shift_left(jnp.ones_like(token_of_row), token_of_row)
    block_of_col = lax.broadcasted_iota(jnp.int32, (1, span), 1) // BLK
    diagonal = lax.broadcasted_iota(jnp.int32, (total_rows, total_rows), 0) == lax.broadcasted_iota(
        jnp.int32, (total_rows, total_rows), 1
    )
    transposed = (((1,), (1,)), ((), ()))

    def attend_group(batch, i):
        g = batch * SIDE + i
        query = jnp.concatenate([q_ref[c, g] for c in range(n_chunks)], axis=0)
        rotary = jnp.concatenate([q_rot_ref[c, g] for c in range(n_chunks)], axis=0)
        scores, key_rows = [], []
        for p in range(n_parts):
            entries = [list_ref[g, p * cap + k] for k in range(cap)]
            latent = jnp.concatenate([keys_ref[p, e // base] for e in entries], axis=0)
            turned = jnp.concatenate([rots_ref[p, e // base] for e in entries], axis=0)
            bits = jnp.zeros((1, span), jnp.int32)
            for k in range(cap):
                bits = jnp.where(block_of_col == k, entries[k] % base, bits)
            score = lax.dot_general(query, latent, transposed, preferred_element_type=jnp.float32)
            score = score + lax.dot_general(
                rotary, turned, transposed, preferred_element_type=jnp.float32
            )
            scores.append(jnp.where((bits & row_bit) != 0, score * scale, EMPTY))
            key_rows.append(latent)
        peak = functools.reduce(
            jnp.maximum, [jnp.max(s, axis=1, keepdims=True) for s in scores]
        )
        total = jnp.zeros_like(peak)
        value = jnp.zeros((total_rows, width), jnp.float32)
        for score, latent in zip(scores, key_rows):
            exponent = jnp.exp(score - peak)
            total = total + jnp.sum(exponent, axis=1, keepdims=True)
            value = value + jnp.dot(
                exponent.astype(jnp.bfloat16), latent, preferred_element_type=jnp.float32
            )
        value = (value / total).astype(jnp.bfloat16)
        for c in range(n_chunks):
            mine[c, g] = value[c * rows : (c + 1) * rows]
        logs[batch, pl.ds(i, 1), :] = jnp.sum(
            jnp.where(diagonal, peak + jnp.log(total), 0.0), axis=0, keepdims=True
        )

    def copies(stage, batch):
        kept = n_chunks >> (stage + 1)
        span_of = pl.ds(batch * SIDE, SIDE)
        pairs = (
            (mine.at[pl.ds(kept, kept), span_of], recvs[stage].at[:, span_of]),
            (logs.at[batch], log_recvs[stage].at[batch]),
        )
        return [
            pltpu.make_async_remote_copy(
                src_ref=source,
                dst_ref=target,
                send_sem=send_sems.at[stage, k, batch],
                recv_sem=recv_sems.at[stage, k, batch],
                device_id={"ctx": peers[stage]},
            )
            for k, (source, target) in enumerate(pairs)
        ]

    def merge(stage, batch):
        kept = n_chunks >> (stage + 1)
        for copy in copies(stage, batch):
            copy.wait()
        own = logs[batch]
        other = pltpu.roll(log_recvs[stage][batch], total_rows - kept * rows, 1)
        top = jnp.maximum(own, other)
        own_share = jnp.exp(own - top)
        other_share = jnp.exp(other - top)
        both = own_share + other_share
        own_share = own_share / both
        other_share = other_share / both
        logs[batch] = top + jnp.log(both)
        used = kept * rows

        def column(shares, i):
            return jnp.sum(
                jnp.where(diagonal[:used], shares[i : i + 1], 0.0), axis=1, keepdims=True
            )

        for i in range(SIDE):
            g = batch * SIDE + i
            left, right = column(own_share, i), column(other_share, i)
            for c in range(kept):
                part = slice(c * rows, (c + 1) * rows)
                value = (
                    mine[c, g].astype(jnp.float32) * left[part]
                    + recvs[stage][c, g].astype(jnp.float32) * right[part]
                ).astype(jnp.bfloat16)
                if stage + 1 < n_stages:
                    mine[c, g] = value
                else:
                    out_ref[g] = value

    def step(time, carry):
        for stage in reversed(range(n_stages)):
            batch = time - LAG * (stage + 1)

            @pl.when((batch >= 0) & (batch < n_batches))
            def _():
                merge(stage, batch)
                if stage + 1 < n_stages:
                    for copy in copies(stage + 1, batch):
                        copy.start()

        @pl.when(time < n_batches)
        def _():
            for i in range(SIDE):
                attend_group(time, i)
            for copy in copies(0, time):
                copy.start()

        return carry

    lax.fori_loop(0, n_batches + LAG * n_stages, step, 0)


def attend_reduce(query_bits, heads, cap, scale, block_list, keys, rots, queries, q_rots):
    n_chunks, groups, rows, width = queries.shape
    n_stages = len(query_bits)
    n_batches = groups // SIDE
    vmem = pl.BlockSpec(memory_space=pltpu.VMEM)
    smem = pl.BlockSpec(memory_space=pltpu.SMEM)
    log_shape = (n_batches, 8, n_chunks * rows)
    return pl.pallas_call(
        functools.partial(reduce_kernel, query_bits, heads, cap, scale),
        out_shape=jax.ShapeDtypeStruct((groups, rows, width), jnp.bfloat16),
        in_specs=[smem] + [vmem] * 4,
        out_specs=vmem,
        scratch_shapes=[
            pltpu.VMEM(queries.shape, jnp.bfloat16),
            pltpu.VMEM(log_shape, jnp.float32),
            *[
                pltpu.VMEM((n_chunks >> (s + 1), groups, rows, width), jnp.bfloat16)
                for s in range(n_stages)
            ],
            *[pltpu.VMEM(log_shape, jnp.float32) for _ in range(n_stages)],
            pltpu.SemaphoreType.DMA((n_stages, 2, n_batches)),
            pltpu.SemaphoreType.DMA((n_stages, 2, n_batches)),
        ],
        compiler_params=pltpu.CompilerParams(
            collective_id=2, has_side_effects=True, vmem_limit_bytes=48 * 2**20
        ),
        name="attend_reduce",
    )(block_list, keys, rots, queries, q_rots)


def project_kernel(bits, tiles, rows_ref, w_ref, out_ref, weights, w_sems, *bufs):
    n_stages = len(bits)
    sends, recvs = bufs[:n_stages], bufs[n_stages : 2 * n_stages]
    send_sems, recv_sems = bufs[2 * n_stages :]
    me = lax.axis_index("ctx")
    upper = [(me // bit) % 2 for bit in bits]
    partner = [me + bit * (1 - 2 * up) for bit, up in zip(bits, upper)]
    width = weights.shape[2]
    loads = [
        pltpu.make_async_copy(
            w_ref.at[:, pl.ds(t * width, width)], weights.at[t], w_sems.at[t]
        )
        for t in range(tiles)
    ]
    for load in loads:
        load.start()
    barrier = pltpu.get_barrier_semaphore()
    for other in partner:
        pl.semaphore_signal(barrier, inc=1, device_id={"ctx": other})
    pl.semaphore_wait(barrier, n_stages)

    def copy_of(k, t):
        return pltpu.make_async_remote_copy(
            src_ref=sends[k].at[t],
            dst_ref=recvs[k].at[t],
            send_sem=send_sems.at[t, k],
            recv_sem=recv_sems.at[t, k],
            device_id={"ctx": partner[k]},
        )

    def send_half(k, t, total):
        half = total.shape[0] // 2
        low, high = total[:half], total[half:]
        sends[k][t] = jnp.where(upper[k] == 1, low, high).astype(jnp.bfloat16)
        copy_of(k, t).start()
        return jnp.where(upper[k] == 1, high, low)

    kept = {}
    for time in range(tiles + LAG * n_stages):
        for k in reversed(range(n_stages)):
            t = time - LAG * (k + 1)
            if 0 <= t < tiles:
                copy_of(k, t).wait()
                total = kept.pop(t) + recvs[k][t].astype(jnp.float32)
                if k + 1 < n_stages:
                    kept[t] = send_half(k + 1, t, total)
                else:
                    out_ref[:, t * width : (t + 1) * width] = total.astype(jnp.bfloat16)
        if time < tiles:
            loads[time].wait()
            total = jnp.dot(rows_ref[...], weights[time], preferred_element_type=jnp.float32)
            kept[time] = send_half(0, time, total)


def project(rows, weight, q_local, n_devices):
    bits = [1 << i for i in range(n_devices.bit_length() - 1)]
    depth, columns = weight.shape
    tiles = max(t for t in range(1, TILES + 1) if columns % (t * 128) == 0)
    width = columns // tiles
    sizes = [rows.shape[0] >> (i + 1) for i in range(len(bits))]
    slots = [pltpu.VMEM((tiles, size, width), jnp.bfloat16) for size in sizes]
    vmem = pl.BlockSpec(memory_space=pltpu.VMEM)
    return pl.pallas_call(
        functools.partial(project_kernel, bits, tiles),
        out_shape=jax.ShapeDtypeStruct((q_local, columns), jnp.bfloat16),
        in_specs=[vmem, pl.BlockSpec(memory_space=pl.ANY)],
        out_specs=vmem,
        scratch_shapes=[
            pltpu.VMEM((tiles, depth, width), jnp.bfloat16),
            pltpu.SemaphoreType.DMA((tiles,)),
            *slots,
            *slots,
            pltpu.SemaphoreType.DMA((tiles, len(bits))),
            pltpu.SemaphoreType.DMA((tiles, len(bits))),
        ],
        compiler_params=pltpu.CompilerParams(
            collective_id=1, has_side_effects=True, vmem_limit_bytes=48 * 2**20
        ),
        name="project",
    )(rows, weight)


def local(
    cache_bits, query_bits, q_latent, q_gain, w_uq, w_uk, w_uv, w_o, latent_cache, kv_scales, selected, counts
):
    n_devices = lax.axis_size("ctx")
    me = lax.axis_index("ctx")
    heads_local, width_content, width_latent = w_uk.shape
    width_rotary = latent_cache.shape[1] - width_latent
    q_local, top_blocks = selected.shape
    blocks_local = latent_cache.shape[0] // BLK
    cap = q_local * top_blocks // n_devices
    groups = n_devices
    row_count = groups * q_local

    live_sel = jnp.arange(top_blocks, dtype=jnp.int32)[None, :] < counts[:, None]
    listed = jnp.where(live_sel, selected, -1)
    keys, rots, queries, q_rots, all_listed = exchange(
        cache_bits, query_bits, n_devices, q_latent, q_gain, listed, w_uq, w_uk, latent_cache, kv_scales
    )
    near_bit, far_bit = cache_bits
    parts_masks = [0, near_bit, far_bit, far_bit | near_bit]
    firsts = jnp.stack([(me ^ mask) * blocks_local for mask in parts_masks])
    held = (firsts[:, None] + jnp.arange(blocks_local, dtype=jnp.int32)[None, :]).reshape(-1)
    member = jnp.any(all_listed[:, :, :, None] == held[None, None, None, :], axis=2).astype(jnp.int32)
    bits = jnp.sum(
        member * lax.shift_left(1, jnp.arange(q_local, dtype=jnp.int32))[None, :, None], axis=1
    ).reshape(groups, len(parts_masks), blocks_local)
    needed = (bits > 0).astype(jnp.int32)
    rank = jnp.cumsum(needed, axis=2) - needed
    entry = jnp.arange(blocks_local, dtype=jnp.int32)[None, None, :] * 2**q_local + bits
    slots = jnp.arange(cap, dtype=jnp.int32)[None, None, :, None]
    slot = (rank[:, :, None, :] == slots) & (needed[:, :, None, :] == 1)
    block_list = jnp.sum(jnp.where(slot, entry[:, :, None, :], 0), axis=3).reshape(groups, -1)

    scale = 1.0 / math.sqrt(width_content + width_rotary)
    latent_out = attend_reduce(
        query_bits, heads_local, cap, scale, block_list, keys, rots, queries, q_rots
    )
    head_out = latent_out.reshape(row_count, heads_local, width_latent)
    head_values = jnp.einsum(
        "qhc,hcv->qhv", head_out, w_uv, preferred_element_type=jnp.float32
    ).astype(jnp.bfloat16)
    n_bits = n_devices.bit_length() - 1
    rows = head_values.reshape((2,) * n_bits + (q_local, -1))
    rows = rows.transpose(tuple(reversed(range(n_bits))) + (n_bits, n_bits + 1))
    return project(rows.reshape(row_count, -1), w_o, q_local, n_devices)


def solution(mesh):
    n_devices = mesh.shape["ctx"]
    all_bits = [1 << i for i in range(n_devices.bit_length() - 1)]
    cache_bits, query_bits = all_bits[:2], all_bits[2:]
    in_specs = (
        P(("groups", "ctx"), None),
        P(),
        P(None, "ctx"),
        P("ctx", None, None),
        P("ctx", None, None),
        P("ctx", None),
        P(("groups", "ctx"), None),
        P(("groups", "ctx"), None),
        P(("groups", "ctx"), None),
        P(("groups", "ctx")),
    )
    out_specs = P(("groups", "ctx"), None)
    return jax.shard_map(
        functools.partial(local, cache_bits, query_bits),
        mesh=mesh,
        in_specs=in_specs,
        out_specs=out_specs,
        check_vma=False,
    )
```

```python
import functools
import math

import jax
import jax.numpy as jnp
from jax import lax
from jax.experimental import pallas as pl
from jax.experimental.pallas import tpu as pltpu
from jax.sharding import PartitionSpec as P

BLK = 64
SIDE = 2
TILES = 4
LAG = 2
SUM_LAG = 2
KEY_PIECES = 8
QUERY_PIECES = 4

norm_eps = 1e-06
rope_base = 10000.0
EMPTY = -1e30


def make_list(owners, cap, blocks, q_local, listed_ref, list_rows):
    total = listed_ref.shape[0]
    groups = math.gcd(total, 16)

    def some_groups(i, carry):
        some = pl.ds(i * groups, groups)
        width = len(owners) * blocks
        lane = lax.broadcasted_iota(jnp.int32, (groups, width), 1)
        inner = lane % blocks
        held = inner
        for p, owner in enumerate(owners):
            held = held + jnp.where(lane // blocks == p, owner * blocks, 0)
        bits = jnp.zeros((groups, width), jnp.int32)
        for t in range(q_local):
            listed = listed_ref[some, t, :]
            member = jnp.zeros((groups, width), jnp.int32)
            for k in range(listed.shape[1]):
                member = jnp.where(listed[:, k : k + 1] == held, 2**t, member)
            bits = bits + member
        needed = jnp.where(bits > 0, 1, 0)
        upto = needed
        reach = 1
        while reach < blocks:
            upto = upto + jnp.where(inner >= reach, pltpu.roll(upto, reach, 1), 0)
            reach *= 2
        rank = upto - needed
        entry = inner * 2**q_local + bits
        result = jnp.zeros((groups, width), jnp.int32)
        for r in range(cap):
            found = jnp.where((rank == r) & (needed == 1), entry, 0)
            reach = blocks // 2
            while reach:
                found = found + pltpu.roll(found, width - reach, 1)
                reach //= 2
            if r:
                found = pltpu.roll(found, r, 1)
            result = jnp.where(inner == r, found, result)
        list_rows[some, :] = result
        return carry

    lax.fori_loop(0, total // groups, some_groups, 0)


def attend_reduce(
    query_bits, heads, cap, scale, list_ref, keys_ref, rots_ref, q_ref, q_rot_ref, out_ref, mine,
    logs, *bufs
):
    n_stages = len(query_bits)
    recvs, log_recvs = bufs[:n_stages], bufs[n_stages : 2 * n_stages]
    send_sems, recv_sems = bufs[2 * n_stages :]
    me = lax.axis_index("ctx")
    n_chunks, groups, rows, width = q_ref.shape
    n_parts = keys_ref.shape[0]
    n_batches = groups // SIDE
    total_rows = n_chunks * rows
    tokens = rows // heads
    base = 2**tokens
    span = cap * BLK
    peers = [me + bit * (1 - 2 * ((me // bit) % 2)) for bit in query_bits]
    token_of_row = (lax.broadcasted_iota(jnp.int32, (total_rows, 1), 0) // heads) % tokens
    row_bit = lax.shift_left(jnp.ones_like(token_of_row), token_of_row)
    block_of_col = lax.broadcasted_iota(jnp.int32, (1, span), 1) // BLK
    diagonal = lax.broadcasted_iota(jnp.int32, (total_rows, total_rows), 0) == lax.broadcasted_iota(
        jnp.int32, (total_rows, total_rows), 1
    )
    transposed = (((1,), (1,)), ((), ()))

    def attend_group(batch, i):
        g = batch * SIDE + i
        query = jnp.concatenate([q_ref[c, g] for c in range(n_chunks)], axis=0)
        rotary = jnp.concatenate([q_rot_ref[c, g] for c in range(n_chunks)], axis=0)
        scores, key_rows = [], []
        for p in range(n_parts):
            entries = [list_ref[g, p * keys_ref.shape[1] + k] for k in range(cap)]
            latent = jnp.concatenate([keys_ref[p, e // base] for e in entries], axis=0)
            turned = jnp.concatenate([rots_ref[p, e // base] for e in entries], axis=0)
            bits = jnp.zeros((1, span), jnp.int32)
            for k in range(cap):
                bits = jnp.where(block_of_col == k, entries[k] % base, bits)
            score = lax.dot_general(query, latent, transposed, preferred_element_type=jnp.float32)
            score = score + lax.dot_general(
                rotary, turned, transposed, preferred_element_type=jnp.float32
            )
            scores.append(jnp.where((bits & row_bit) != 0, score * scale, EMPTY))
            key_rows.append(latent)
        peak = functools.reduce(
            jnp.maximum, [jnp.max(s, axis=1, keepdims=True) for s in scores]
        )
        total = jnp.zeros_like(peak)
        value = jnp.zeros((total_rows, width), jnp.float32)
        for score, latent in zip(scores, key_rows):
            exponent = jnp.exp(score - peak)
            total = total + jnp.sum(exponent, axis=1, keepdims=True)
            value = value + jnp.dot(
                exponent.astype(jnp.bfloat16), latent, preferred_element_type=jnp.float32
            )
        value = (value / total).astype(jnp.bfloat16)
        for c in range(n_chunks):
            mine[c, g] = value[c * rows : (c + 1) * rows]
        logs[batch, pl.ds(i, 1), :] = jnp.sum(
            jnp.where(diagonal, peak + jnp.log(total), 0.0), axis=0, keepdims=True
        )

    def copies(stage, batch):
        kept = n_chunks >> (stage + 1)
        span_of = pl.ds(batch * SIDE, SIDE)
        pairs = (
            (mine.at[pl.ds(kept, kept), span_of], recvs[stage].at[:, span_of]),
            (logs.at[batch], log_recvs[stage].at[batch]),
        )
        return [
            pltpu.make_async_remote_copy(
                src_ref=source,
                dst_ref=target,
                send_sem=send_sems.at[stage, k, batch],
                recv_sem=recv_sems.at[stage, k, batch],
                device_id={"ctx": peers[stage]},
            )
            for k, (source, target) in enumerate(pairs)
        ]

    def merge(stage, batch):
        kept = n_chunks >> (stage + 1)
        for copy in copies(stage, batch):
            copy.wait()
        own = logs[batch]
        other = pltpu.roll(log_recvs[stage][batch], total_rows - kept * rows, 1)
        top = jnp.maximum(own, other)
        own_share = jnp.exp(own - top)
        other_share = jnp.exp(other - top)
        both = own_share + other_share
        own_share = own_share / both
        other_share = other_share / both
        logs[batch] = top + jnp.log(both)
        used = kept * rows

        def column(shares, i):
            return jnp.sum(
                jnp.where(diagonal[:used], shares[i : i + 1], 0.0), axis=1, keepdims=True
            )

        for i in range(SIDE):
            g = batch * SIDE + i
            left, right = column(own_share, i), column(other_share, i)
            for c in range(kept):
                part = slice(c * rows, (c + 1) * rows)
                value = (
                    mine[c, g].astype(jnp.float32) * left[part]
                    + recvs[stage][c, g].astype(jnp.float32) * right[part]
                ).astype(jnp.bfloat16)
                if stage + 1 < n_stages:
                    mine[c, g] = value
                else:
                    out_ref[g] = value

    def step(time, carry):
        for stage in reversed(range(n_stages)):
            batch = time - LAG * (stage + 1)

            @pl.when((batch >= 0) & (batch < n_batches))
            def _():
                merge(stage, batch)
                if stage + 1 < n_stages:
                    for copy in copies(stage + 1, batch):
                        copy.start()

        @pl.when(time < n_batches)
        def _():
            for i in range(SIDE):
                attend_group(time, i)
            for copy in copies(0, time):
                copy.start()

        return carry

    lax.fori_loop(0, n_batches + LAG * n_stages, step, 0)


def attend_kernel(
    cache_bits, query_bits, cap, scale, q_ref, gain_ref, sel_ref, scales_ref, w_uq_ref, w_uk_ref,
    cache_ref, out_ref, keys_ref, rots_ref, q_out_ref, q_rot_ref, sel_out_ref, q_in, gain, scales,
    raw, w_uq, w_uk, normed, lat, rows_x, rows_q, rows_r, q_pack, list_rows, list_ref,
    load_sems, gather_send, gather_recv, key_send, key_recv, q_send, q_recv, *reduce_refs,
):
    n_devices = lat.shape[0]
    me = lax.axis_index("ctx")
    near_bit, far_bit = cache_bits
    q_local, width_q = q_ref.shape
    width_row, span = raw.shape
    n_tiles = scales_ref.shape[0]
    heads, width_content, width_latent = w_uk.shape
    width_rotary = width_row - width_latent
    width_head = width_content + width_rotary
    _, blocks, blk, _ = keys_ref.shape
    n_chunks, groups, rows, _ = q_out_ref.shape
    key_step = blocks // KEY_PIECES
    q_step = groups // QUERY_PIECES
    key_span = span // KEY_PIECES
    tokens = n_devices * q_local
    half = width_rotary // 2

    def peer(bit):
        return me + bit * (1 - 2 * ((me // bit) % 2))

    def key_load(i):
        part = pl.ds(i * key_span, key_span)
        return pltpu.make_async_copy(
            cache_ref.at[:width_latent, part], raw.at[:width_latent, part], load_sems.at[i]
        )

    others = [
        pltpu.make_async_copy(source, target, load_sems.at[KEY_PIECES + k])
        for k, (source, target) in enumerate(
            (
                (q_ref, q_in),
                (gain_ref, gain),
                (scales_ref, scales),
                (cache_ref.at[width_latent:], raw.at[width_latent:]),
                (w_uq_ref, w_uq),
                (w_uk_ref, w_uk),
            )
        )
    ]
    q_load, gain_load, scales_load, rot_load, w_uq_load, w_uk_load = others
    q_load.start()
    gain_load.start()
    scales_load.start()
    rot_load.start()
    for i in range(KEY_PIECES):
        key_load(i).start()
    w_uq_load.start()
    w_uk_load.start()
    barrier = pltpu.get_barrier_semaphore()
    for d in range(1, n_devices):
        pl.semaphore_signal(barrier, inc=1, device_id={"ctx": (me + d) % n_devices})

    q_load.wait()
    gain_load.wait()
    latent = q_in[...].astype(jnp.float32)
    mean = jnp.mean(latent * latent, axis=1, keepdims=True)
    normed[...] = (latent * lax.rsqrt(mean + norm_eps) * gain[...]).astype(jnp.bfloat16)
    rot_load.wait()
    halfway = span // 2
    stacked = jnp.concatenate(
        [raw[width_latent:, :halfway], raw[width_latent:, halfway:]], axis=0
    ).astype(jnp.float32)
    rots_ref[0, : blocks // 2] = stacked.T.astype(jnp.bfloat16).reshape(blocks // 2, blk, -1)

    def key_copy(kind, i):
        source, target, bit = ((0, 1, near_bit), (0, 2, far_bit), (2, 3, near_bit))[kind]
        if i == KEY_PIECES:
            ref, piece = rots_ref, pl.ds(0, blocks // 2)
        else:
            ref, piece = keys_ref, pl.ds(i * key_step, key_step)
        return pltpu.make_async_remote_copy(
            src_ref=ref.at[source, piece],
            dst_ref=ref.at[target, piece],
            send_sem=key_send.at[kind, i],
            recv_sem=key_recv.at[kind, i],
            device_id={"ctx": peer(bit)},
        )

    def scale_piece(i):
        key_load(i).wait()
        part = slice(i * key_span, (i + 1) * key_span)
        deep = width_latent // n_tiles
        for c in range(n_tiles):
            strip = (
                raw[c * deep : (c + 1) * deep, part].astype(jnp.float32) * scales[c : c + 1, part]
            )
            keys_ref[0, i * key_step : (i + 1) * key_step, :, c * deep : (c + 1) * deep] = (
                strip.T.astype(jnp.bfloat16).reshape(key_step, blk, deep)
            )

    pl.semaphore_wait(barrier, n_devices - 1)
    gathers = []
    for d in range(1, n_devices):
        for k, (source, target) in enumerate(((normed, lat), (sel_ref, sel_out_ref))):
            gathers.append(
                pltpu.make_async_remote_copy(
                    src_ref=source,
                    dst_ref=target.at[me],
                    send_sem=gather_send.at[k, d],
                    recv_sem=gather_recv.at[k, d],
                    device_id={"ctx": (me + d) % n_devices},
                )
            )
    for copy in gathers:
        copy.start()
    key_copy(1, KEY_PIECES).start()
    key_copy(0, KEY_PIECES).start()
    lat[me] = normed[...]
    sel_out_ref[me] = sel_ref[...]
    scales_load.wait()
    for i in range(KEY_PIECES):
        scale_piece(i)
        key_copy(1, i).start()
        key_copy(0, i).start()
    lane = lax.broadcasted_iota(jnp.int32, (tokens, width_rotary), 1)
    position = lax.broadcasted_iota(jnp.int32, (tokens, width_rotary), 0).astype(jnp.float32)
    frequency = jnp.exp((lane % half).astype(jnp.float32) * (-2.0 * math.log(rope_base) / width_rotary))
    cosine = jnp.cos(position * frequency)
    sine = jnp.sin(position * frequency) * jnp.where(lane < half, -1.0, 1.0)
    w_uq_load.wait()
    w_uk_load.wait()
    for copy in gathers:
        copy.wait()
    for d in range(n_devices):
        rows_x[d * q_local : (d + 1) * q_local] = lat[d].astype(jnp.float32)
    projected = jnp.dot(
        rows_x[...].astype(jnp.bfloat16), w_uq[...], preferred_element_type=jnp.float32
    )
    for h in range(heads):
        head = projected[:, h * width_head : (h + 1) * width_head]
        rotary = head[:, width_content:]
        swapped = jnp.concatenate([rotary[:, half:], rotary[:, :half]], axis=1)
        rows_r[:, h, :] = rotary * cosine + swapped * sine
    pairs = jnp.concatenate([rows_r[: tokens // 2], rows_r[tokens // 2 :]], axis=2)
    q_pack[0] = pairs.reshape(groups // 2, rows, 2 * width_rotary).astype(jnp.bfloat16)

    stages = [(i, bit) for i, bit in enumerate(reversed(query_bits))]

    def q_copy(stage, source, j):
        target = 2**stage + source
        if j == QUERY_PIECES:
            ref, piece = q_pack, pl.ds(0, groups // 2)
        else:
            ref, piece = q_out_ref, pl.ds(j * q_step, q_step)
        return pltpu.make_async_remote_copy(
            src_ref=ref.at[source, piece],
            dst_ref=ref.at[target, piece],
            send_sem=q_send.at[target, j],
            recv_sem=q_recv.at[target, j],
            device_id={"ctx": peer(stages[stage][1])},
        )

    for h in range(heads):
        rows_q[:, h, :] = jnp.dot(
            projected[:, h * width_head : h * width_head + width_content].astype(jnp.bfloat16),
            w_uk[h],
            preferred_element_type=jnp.float32,
        )
    for j in range(QUERY_PIECES):
        first = j * q_step
        q_out_ref[0, first : first + q_step] = (
            rows_q[first * q_local : (first + q_step) * q_local]
            .reshape(q_step, rows, width_latent)
            .astype(jnp.bfloat16)
        )
        for stage, _ in stages:
            q_copy(stage, 0, j).start()
    for stage, _ in stages:
        q_copy(stage, 0, QUERY_PIECES).start()

    low_lane = lax.broadcasted_iota(jnp.int32, (groups // 2, rows, 2 * width_rotary), 2) < width_rotary

    def unpack_query(slot):
        pair = q_pack[slot].astype(jnp.float32)
        rolled = jnp.concatenate([pair[:, :, width_rotary:], pair[:, :, :width_rotary]], axis=2)
        q_rot_ref[slot, : groups // 2] = jnp.where(low_lane, pair, 0.0).astype(jnp.bfloat16)
        q_rot_ref[slot, groups // 2 :] = jnp.where(low_lane, rolled, 0.0).astype(jnp.bfloat16)

    def unpack_rots(slot):
        pair = rots_ref[slot, : blocks // 2].astype(jnp.float32)
        rolled = jnp.concatenate([pair[:, :, width_rotary:], pair[:, :, :width_rotary]], axis=2)
        rots_ref[slot, blocks // 2 :] = rolled.astype(jnp.bfloat16)

    owners = [me, peer(near_bit), peer(far_bit), peer(near_bit) + peer(far_bit) - me]
    make_list(owners, cap, blocks, q_local, sel_out_ref, list_rows)
    list_load = pltpu.make_async_copy(list_rows, list_ref, load_sems.at[KEY_PIECES + 6])
    list_load.start()
    unpack_query(0)
    unpack_rots(0)
    key_copy(0, KEY_PIECES).wait_recv()
    unpack_rots(1)
    arrivals = [(0.0, "key", KEY_PIECES, 0)]
    for i in range(KEY_PIECES):
        arrivals.append(((i + 1.0) / KEY_PIECES, "key", i, 0))
    for j in range(QUERY_PIECES + 1):
        for slot in range(1, n_chunks):
            at = 0.15 + 0.85 * (slot * QUERY_PIECES + j + 1.0) / (n_chunks * QUERY_PIECES)
            arrivals.append((at, "query", slot, j))
    for _, what, a, b in sorted(arrivals):
        if what == "key":
            key_copy(1, a).wait_recv()
            key_copy(2, a).start()
            if a == KEY_PIECES:
                unpack_rots(2)
        else:
            stage = a.bit_length() - 1
            q_copy(stage, a - 2**stage, b).wait_recv()
            for later in range(stage + 1, len(stages)):
                q_copy(later, a, b).start()
            if b == QUERY_PIECES:
                unpack_query(a)
    key_copy(2, KEY_PIECES).wait_recv()
    unpack_rots(3)
    for i in range(KEY_PIECES):
        key_copy(0, i).wait_recv()
        key_copy(2, i).wait_recv()
    list_load.wait()
    attend_reduce(
        query_bits, heads, cap, scale, list_ref, keys_ref, rots_ref, q_out_ref, q_rot_ref, out_ref,
        *reduce_refs
    )
    for i in range(KEY_PIECES + 1):
        for kind in range(3):
            key_copy(kind, i).wait_send()
    for j in range(QUERY_PIECES + 1):
        for slot in range(1, n_chunks):
            stage = slot.bit_length() - 1
            q_copy(stage, slot - 2**stage, j).wait_send()


def attend(
    cache_bits, query_bits, cap, scale, n_devices, q_latent, q_gain, listed, w_uq, w_uk, latent_cache,
    kv_scales
):
    q_local, width_q = q_latent.shape
    heads, _, width_latent = w_uk.shape
    span, width_row = latent_cache.shape
    blocks = span // BLK
    tokens = n_devices * q_local
    groups = n_devices
    n_stages = len(query_bits)
    n_chunks = 2**n_stages
    rows = q_local * heads
    width_rotary = width_row - width_latent
    n_batches = groups // SIDE
    log_shape = (n_batches, 8, n_chunks * rows)
    vmem = pl.BlockSpec(memory_space=pltpu.VMEM)
    any_space = pl.BlockSpec(memory_space=pl.ANY)
    half_keys = pltpu.VMEM((4, blocks, BLK, 2 * width_rotary), jnp.bfloat16)
    return pl.pallas_call(
        functools.partial(attend_kernel, cache_bits, query_bits, cap, scale),
        out_shape=jax.ShapeDtypeStruct((groups, rows, width_latent), jnp.bfloat16),
        in_specs=[any_space] * 2 + [vmem] + [any_space] * 4,
        out_specs=vmem,
        scratch_shapes=[
            pltpu.VMEM((4, blocks, BLK, width_latent), jnp.bfloat16),
            half_keys,
            pltpu.VMEM((n_chunks, groups, rows, width_latent), jnp.bfloat16),
            pltpu.VMEM((n_chunks, groups, rows, 2 * width_rotary), jnp.bfloat16),
            pltpu.VMEM((n_devices,) + listed.shape, jnp.int32),
            pltpu.VMEM(q_latent.shape, jnp.bfloat16),
            pltpu.VMEM((1, width_q), jnp.float32),
            pltpu.VMEM(kv_scales.shape[::-1], jnp.float32),
            pltpu.VMEM((width_row, span), jnp.bfloat16),
            pltpu.VMEM(w_uq.shape, jnp.bfloat16),
            pltpu.VMEM(w_uk.shape, jnp.bfloat16),
            pltpu.VMEM(q_latent.shape, jnp.bfloat16),
            pltpu.VMEM((n_devices,) + q_latent.shape, jnp.bfloat16),
            pltpu.VMEM((tokens, width_q), jnp.float32),
            pltpu.VMEM((tokens, heads, width_latent), jnp.float32),
            pltpu.VMEM((tokens, heads, width_rotary), jnp.float32),
            pltpu.VMEM((n_chunks, groups // 2, rows, 2 * width_rotary), jnp.bfloat16),
            pltpu.VMEM((groups, 4 * blocks), jnp.int32),
            pltpu.SMEM((groups, 4 * blocks), jnp.int32),
            pltpu.SemaphoreType.DMA((KEY_PIECES + 7,)),
            pltpu.SemaphoreType.DMA((2, n_devices)),
            pltpu.SemaphoreType.DMA((2, n_devices)),
            pltpu.SemaphoreType.DMA((3, KEY_PIECES + 1)),
            pltpu.SemaphoreType.DMA((3, KEY_PIECES + 1)),
            pltpu.SemaphoreType.DMA((n_chunks, QUERY_PIECES + 1)),
            pltpu.SemaphoreType.DMA((n_chunks, QUERY_PIECES + 1)),
            pltpu.VMEM((n_chunks, groups, rows, width_latent), jnp.bfloat16),
            pltpu.VMEM(log_shape, jnp.float32),
            *[
                pltpu.VMEM((n_chunks >> (s + 1), groups, rows, width_latent), jnp.bfloat16)
                for s in range(n_stages)
            ],
            *[pltpu.VMEM(log_shape, jnp.float32) for _ in range(n_stages)],
            pltpu.SemaphoreType.DMA((n_stages, 2, n_batches)),
            pltpu.SemaphoreType.DMA((n_stages, 2, n_batches)),
        ],
        compiler_params=pltpu.CompilerParams(
            collective_id=0, has_side_effects=True, vmem_limit_bytes=58 * 2**20
        ),
        name="attend",
    )(q_latent, q_gain[None, :], listed, kv_scales.T, w_uq, w_uk, latent_cache.T)


def project_kernel(bits, tiles, rows_ref, w_ref, out_ref, weights, w_sems, *bufs):
    n_stages = len(bits)
    sends, recvs = bufs[:n_stages], bufs[n_stages : 2 * n_stages]
    send_sems, recv_sems = bufs[2 * n_stages :]
    me = lax.axis_index("ctx")
    upper = [(me // bit) % 2 for bit in bits]
    partner = [me + bit * (1 - 2 * up) for bit, up in zip(bits, upper)]
    width = weights.shape[2]
    loads = [
        pltpu.make_async_copy(
            w_ref.at[:, pl.ds(t * width, width)], weights.at[t], w_sems.at[t]
        )
        for t in range(tiles)
    ]
    for load in loads:
        load.start()
    barrier = pltpu.get_barrier_semaphore()
    for other in partner:
        pl.semaphore_signal(barrier, inc=1, device_id={"ctx": other})
    pl.semaphore_wait(barrier, n_stages)

    def copy_of(k, t):
        return pltpu.make_async_remote_copy(
            src_ref=sends[k].at[t],
            dst_ref=recvs[k].at[t],
            send_sem=send_sems.at[t, k],
            recv_sem=recv_sems.at[t, k],
            device_id={"ctx": partner[k]},
        )

    def send_half(k, t, total):
        half = total.shape[0] // 2
        low, high = total[:half], total[half:]
        sends[k][t] = jnp.where(upper[k] == 1, low, high).astype(jnp.bfloat16)
        copy_of(k, t).start()
        return jnp.where(upper[k] == 1, high, low)

    kept = {}
    for time in range(tiles + SUM_LAG * n_stages):
        for k in reversed(range(n_stages)):
            t = time - SUM_LAG * (k + 1)
            if 0 <= t < tiles:
                copy_of(k, t).wait()
                total = kept.pop(t) + recvs[k][t].astype(jnp.float32)
                if k + 1 < n_stages:
                    kept[t] = send_half(k + 1, t, total)
                else:
                    out_ref[:, t * width : (t + 1) * width] = total.astype(jnp.bfloat16)
        if time < tiles:
            loads[time].wait()
            total = jnp.dot(rows_ref[...], weights[time], preferred_element_type=jnp.float32)
            kept[time] = send_half(0, time, total)


def project(rows, weight, q_local, n_devices):
    bits = [1 << i for i in range(n_devices.bit_length() - 1)]
    depth, columns = weight.shape
    tiles = max(t for t in range(1, TILES + 1) if columns % (t * 128) == 0)
    width = columns // tiles
    sizes = [rows.shape[0] >> (i + 1) for i in range(len(bits))]
    slots = [pltpu.VMEM((tiles, size, width), jnp.bfloat16) for size in sizes]
    vmem = pl.BlockSpec(memory_space=pltpu.VMEM)
    return pl.pallas_call(
        functools.partial(project_kernel, bits, tiles),
        out_shape=jax.ShapeDtypeStruct((q_local, columns), jnp.bfloat16),
        in_specs=[vmem, pl.BlockSpec(memory_space=pl.ANY)],
        out_specs=vmem,
        scratch_shapes=[
            pltpu.VMEM((tiles, depth, width), jnp.bfloat16),
            pltpu.SemaphoreType.DMA((tiles,)),
            *slots,
            *slots,
            pltpu.SemaphoreType.DMA((tiles, len(bits))),
            pltpu.SemaphoreType.DMA((tiles, len(bits))),
        ],
        compiler_params=pltpu.CompilerParams(
            collective_id=1, has_side_effects=True, vmem_limit_bytes=48 * 2**20
        ),
        name="project",
    )(rows, weight)


def local(
    cache_bits, query_bits, q_latent, q_gain, w_uq, w_uk, w_uv, w_o, latent_cache, kv_scales, selected, counts
):
    n_devices = lax.axis_size("ctx")
    heads_local, width_content, width_latent = w_uk.shape
    width_rotary = latent_cache.shape[1] - width_latent
    q_local, top_blocks = selected.shape
    cap = q_local * top_blocks // n_devices
    row_count = n_devices * q_local

    live_sel = jnp.arange(top_blocks, dtype=jnp.int32)[None, :] < counts[:, None]
    listed = jnp.where(live_sel, selected, -1)
    scale = 1.0 / math.sqrt(width_content + width_rotary)
    latent_out = attend(
        cache_bits, query_bits, cap, scale, n_devices, q_latent, q_gain, listed, w_uq, w_uk,
        latent_cache, kv_scales
    )
    head_out = latent_out.reshape(row_count, heads_local, width_latent)
    head_values = jnp.einsum(
        "qhc,hcv->qhv", head_out, w_uv, preferred_element_type=jnp.float32
    ).astype(jnp.bfloat16)
    n_bits = n_devices.bit_length() - 1
    rows = head_values.reshape((2,) * n_bits + (q_local, -1))
    rows = rows.transpose(tuple(reversed(range(n_bits))) + (n_bits, n_bits + 1))
    return project(rows.reshape(row_count, -1), w_o, q_local, n_devices)


def solution(mesh):
    n_devices = mesh.shape["ctx"]
    all_bits = [1 << i for i in range(n_devices.bit_length() - 1)]
    cache_bits, query_bits = all_bits[:2], all_bits[2:]
    in_specs = (
        P(("groups", "ctx"), None),
        P(),
        P(None, "ctx"),
        P("ctx", None, None),
        P("ctx", None, None),
        P("ctx", None),
        P(("groups", "ctx"), None),
        P(("groups", "ctx"), None),
        P(("groups", "ctx"), None),
        P(("groups", "ctx")),
    )
    out_specs = P(("groups", "ctx"), None)
    return jax.shard_map(
        functools.partial(local, cache_bits, query_bits),
        mesh=mesh,
        in_specs=in_specs,
        out_specs=out_specs,
        check_vma=False,
    )
```
